128 devices in a mesh: band: 4 (over y), patch: 32 (over x, z, core).
Axes of the slice: x: 4, y: 4, z: 4, core: 2. Of those that a mesh axis runs over, the one named last changes fastest.
Arguments:
- images: float32 [4, 1024, 168, 168], P('band', 'patch'), may hold values from -48 to 48
- coeffs: bfloat16 [4, 1024, 3, 128, 128], P('band', 'patch'), may hold values from 0.29882812 to 1.5
- inverse_var: float32 [4, 1024, 128, 128], P('band', 'patch'), may hold values from 0.3 to 3
- bad_lines: int32 [4, 1024, 2], P('band', 'patch'), may hold values from 0 to 127
- destinations: int32 [4, 1024, 1], P('band', 'patch'), may hold values from 0 to 31; in each aligned block of 32 rows (0 to 31, 32 to 63, ..., all dimensions but the last counted through in order) at most 2 rows name the same one
- tile_slots: int32 [4, 1024], P('band', 'patch'), may hold values from 0 to 15
Outputs:
- coadd: float32 [4, 32, 256, 1024], P('band', 'patch')
- detection: float32 [32, 256, 1024], P('patch', 'band')
The draws below stay inside these ranges and needn't reach their ends.
Inputs may be any that keep to these rules, and one draw needn't show every extreme that they name: `destinations`: among the 32 pieces of one band held by one index of patch (aligned blocks), no patch is named more than 2 times, a bound that some block reaches.
All inputs are finite; a program needn't handle non-finite values.
Results may differ from the reference program's by a relative error of at most 0.00035.
Values sent between devices are 32-bit elements; how exact they have to be, the bound alone decides.
No kernel may reach another device: no remote copies, remote signals or barrier semaphores. Data moves between devices by JAX's collectives and lax.ppermute only.
A program may use at most 192 MiB of HBM per device.

```python
import math
import jax
import jax.numpy as jnp
import numpy as np
from jax import lax

TILE = 128
RADIUS = 20
KERNELS = 3
TILES_X = 8
TILES_Y = 2
PIECES_DEV = 32
CAP = 2
BANDS = 4
PATCHES = 32
PIECES = 1024


def set_ends(result, own_key, smallest, largest):
    longest = result.shape.index(max(result.shape))
    spots = []
    for shift in (0, 1):
        where = [jax.random.randint(jax.random.fold_in(own_key, axis), (), 0, length) for axis, length in enumerate(result.shape)]
        where[longest] = (where[longest] + shift) % result.shape[longest]
        spots.append(tuple(where))
    return result.at[spots[0]].set(smallest).at[spots[1]].set(largest)


def steps_of(rng, shape, shards, low, top_value):
    level, own = 1.0, jax.random.fold_in(rng, 6)
    for position, shards_of in shards:
        heights = jnp.exp(jax.random.uniform(jax.random.fold_in(own, position), (shards_of,), jnp.float32, low / len(shards), top_value / len(shards)))
        level = level * jnp.repeat(heights, shape[position] // shards_of).reshape([-1 if axis == position else 1 for axis in range(len(shape))])
    return level


def deal_out(stream_key, own, number, rows, count, top, bound, skew):
    ranking = jax.random.permutation(stream_key, count)
    crowded, ordinary = shares(count, rows * top, bound, skew, True), shares(count, rows * top, bound, skew, False)
    places = jnp.arange(count)

    def named(lengths, turn):
        used = int((lengths > 0).sum())
        fixed = max(1, used // 4)
        moved = fixed + (places - fixed + turn * (used - fixed)) % max(1, count - fixed)
        return jnp.zeros((count,), jnp.int32).at[ranking[jnp.where(places < fixed, places, moved)]].set(jnp.asarray(lengths, jnp.int32))

    lengths = jnp.where(number % 4 == 0, named(crowded, number // 4), named(ordinary, number - number // 4 - 1))
    mixed = jax.random.permutation(jax.random.fold_in(own, 3), count)
    giver, sink = mixed[0:count // 2 * 2:2], mixed[1:count // 2 * 2:2]
    room = jnp.minimum(lengths[giver] - 1, bound - lengths[sink]) // 2
    room = jnp.where((giver == ranking[0]) | (sink == ranking[0]) | (lengths[sink] == 0), 0, jnp.maximum(room, 0))
    moved = jax.random.randint(jax.random.fold_in(own, 4), (count // 2,), 0, 1 << 20) % (room + 1)
    lengths = lengths.at[giver].add(-moved).at[sink].add(moved)
    members = jnp.searchsorted(jnp.cumsum(lengths), jnp.arange(rows * top), side="right").astype(jnp.int32)
    table = members.reshape(top, rows).T
    table = table[jax.random.permutation(jax.random.fold_in(own, 1), rows)]
    turn = jax.random.randint(jax.random.fold_in(own, 2), (rows, 1), 0, top)
    return jnp.take_along_axis(table, (jnp.arange(top)[None, :] + turn) % top, axis=1)


def shares(number_of, total, bound, lean, full):
    weights = [(1 << 20) // math.isqrt(rank ** lean) + 1 for rank in range(1, number_of + 1)]
    largest = bound if full else min(bound, max(-(-total // number_of), total * weights[0] // sum(weights)))
    least = 1 if total - largest >= number_of - 1 else 0
    holding, rest = [largest] + [least] * (number_of - 1), total - largest - least * (number_of - 1)
    while rest > 0:
        free = [i for i in range(1, number_of) if holding[i] < largest] or [i for i in range(1, number_of) if holding[i] < bound]
        mass, budget = sum([weights[i] for i in free]), rest
        for i in free:
            more = min(bound - holding[i], max(1, budget * weights[i] // mass), rest)
            holding[i] = holding[i] + more
            rest = rest - more
    return np.array(holding)


def normal_values(rng, extent, width, reach, cuts=(), held_as=jnp.bfloat16):
    result = jax.random.normal(rng, extent, jnp.float32) * width
    if len(cuts) > 0:
        result = steps_of(rng, extent, cuts, -0.22, 0.18) * result
    return jnp.clip(result, min=-reach, max=reach).astype(held_as)


def setup_inputs(seed: int = 0) -> dict:
    key_list = jax.random.split(jax.random.key(seed), 7)
    images = normal_values(key_list[0], (BANDS, PIECES, TILE + 2 * RADIUS, TILE + 2 * RADIUS), 8.0, 48.0, ((0, 4), (1, 32)), jnp.float32)
    coeffs = jnp.clip(0.29882812 + 1.2011719 * jax.random.uniform(key_list[1], (BANDS, PIECES, KERNELS, TILE, TILE), jnp.float32) ** steps_of(key_list[1], (BANDS, PIECES, KERNELS, TILE, TILE), ((0, 4), (1, 32)), -0.2, 0.2), 0.29882812, 1.5).astype(jnp.bfloat16)
    inverse_var = jnp.clip(jnp.exp(math.log(3.0) - 2.3025851 * jax.random.uniform(key_list[2], (BANDS, PIECES, TILE, TILE), jnp.float32) ** steps_of(key_list[2], (BANDS, PIECES, TILE, TILE), ((0, 4), (1, 32)), -0.2, 0.2)), 0.3, 3.0)
    bad_lines = set_ends(jax.random.randint(key_list[3], (BANDS, PIECES, 2), 0, TILE), jax.random.fold_in(key_list[3], 1), 0, TILE - 1).astype(jnp.int32)
    destinations_keys = jax.random.split(jax.random.fold_in(key_list[4], 1), BANDS * PIECES // PIECES_DEV)
    destinations_turns = jax.random.permutation(jax.random.fold_in(key_list[4], 3), BANDS * PIECES // PIECES_DEV)
    destinations = jax.vmap(lambda own, number: deal_out(jax.random.fold_in(key_list[4], 2), own, number, PIECES_DEV, PATCHES, 1, CAP, 2))(destinations_keys, destinations_turns).reshape((BANDS, PIECES, 1))
    tile_slots = set_ends(jax.random.randint(key_list[5], (BANDS, PIECES), 0, TILES_X * TILES_Y), jax.random.fold_in(key_list[5], 1), 0, (TILES_X * TILES_Y) - 1).astype(jnp.int32)
    return {"images": images, "coeffs": coeffs, "inverse_var": inverse_var, "bad_lines": bad_lines, "destinations": destinations, "tile_slots": tile_slots}


HIGHEST = lax.Precision.HIGHEST
FRACTIONS = (0.12, 0.25, 0.45)
FLOOR = 0.5


def kernel_bands(tile_side, half_taps):
    offset = jnp.arange(tile_side + 2 * half_taps, dtype=jnp.int32)[None, :] - jnp.arange(tile_side, dtype=jnp.int32)[:, None]
    inside = (offset >= 0) & (offset <= 2 * half_taps)
    centred = (offset - half_taps).astype(jnp.float32)
    tap_offsets = (jnp.arange(2 * half_taps + 1, dtype=jnp.int32) - half_taps).astype(jnp.float32)
    matrices = []
    for fraction in FRACTIONS:
        sigma_width = fraction * half_taps
        tap_total = jnp.sum(jnp.exp(-0.5 * (tap_offsets / sigma_width) ** 2))
        matrices.append(jnp.where(inside, jnp.exp(-0.5 * (centred / sigma_width) ** 2) / tap_total, 0.0))
    return jnp.stack(matrices)


def match_pieces(images, coeffs, bands):
    rows_done = jnp.einsum("kyi,pij->pkyj", bands, images, precision=HIGHEST)
    smoothed = jnp.einsum("pkyj,kxj->pkyx", rows_done, bands, precision=HIGHEST)
    return jnp.sum(coeffs * smoothed, axis=1)


def reference(images, coeffs, inverse_var, bad_lines, destinations, tile_slots):
    bands = kernel_bands(TILE, RADIUS)
    line_index = jnp.arange(TILE, dtype=jnp.int32)
    tiles_all = TILES_Y * TILES_X
    coadd_list = []
    detection = jnp.zeros((PATCHES, TILES_Y * TILE, TILES_X * TILE), jnp.float32)
    for band_index in range(BANDS):
        matched = match_pieces(images[band_index], coeffs[band_index].astype(jnp.float32), bands)
        lines = bad_lines[band_index]
        keep_pixel = (line_index[None, :, None] != lines[:, 0][:, None, None]) & (line_index[None, None, :] != lines[:, 1][:, None, None])
        weight = jnp.where(keep_pixel, inverse_var[band_index], 0.0)
        segment_ids = (destinations[band_index, :, 0] * tiles_all + tile_slots[band_index]).astype(jnp.int32)
        numer_tiles = jax.ops.segment_sum(weight * matched, segment_ids, num_segments=PATCHES * tiles_all)
        denom_tiles = jax.ops.segment_sum(weight, segment_ids, num_segments=PATCHES * tiles_all)

        def assemble(planes):
            return planes.reshape(PATCHES, TILES_Y, TILES_X, TILE, TILE).transpose(0, 1, 3, 2, 4).reshape(PATCHES, TILES_Y * TILE, TILES_X * TILE)

        numerator = assemble(numer_tiles)
        denominator = assemble(denom_tiles)
        coadd = numerator / jnp.maximum(denominator, FLOOR)
        coadd_list.append(coadd)
        detection = detection + numerator * coadd
    return jnp.stack(coadd_list), detection
```

```python
import jax
import jax.numpy as jnp
import ml_dtypes
import numpy as np
from jax import lax
from jax.experimental import pallas as pl
from jax.experimental.pallas import tpu as pltpu
from jax.sharding import PartitionSpec as P

TILES_X = 8
TILES_Y = 2
TILES = TILES_X * TILES_Y
FRACTIONS = (0.12, 0.25, 0.45)
KERNELS = len(FRACTIONS)
FLOOR = 0.5
EVERY = ("band", "patch")
GROUP = 8
LANES = 128
VMEM_LIMIT = 60 << 20
PLACE_LIMIT = 24 << 20


def split_pair(values):
    high = values.astype(jnp.bfloat16)
    low = (values - high.astype(jnp.float32)).astype(jnp.bfloat16)
    return high, low


def kernel_bands(side, taps):
    offset = np.arange(side + 2 * taps)[None, :] - np.arange(side)[:, None]
    inside = (offset >= 0) & (offset <= 2 * taps)
    reach = np.arange(2 * taps + 1) - taps
    pairs = []
    for fraction in FRACTIONS:
        width = fraction * taps
        total = np.exp(-0.5 * (reach / width) ** 2).sum()
        full = np.where(inside, np.exp(-0.5 * ((offset - taps) / width) ** 2) / total, 0.0)
        full = full.astype(np.float32)
        high = full.astype(ml_dtypes.bfloat16)
        low = (full - high.astype(np.float32)).astype(ml_dtypes.bfloat16)
        pairs.append((high, low))
    columns = np.concatenate([h.T for h, _ in pairs] + [l.T for _, l in pairs], axis=1)
    rows = np.stack([np.concatenate(pair, axis=0) for pair in pairs])
    return columns, rows


def match_body(lines, image_ref, coeff_ref, inverse_ref, columns_ref, rows_ref, out_ref, scratch):
    side = inverse_ref.shape[-1]
    half = side // 2
    group = pl.program_id(0)
    row_index = lax.broadcasted_iota(jnp.int32, (side, side), 0)
    lane_index = lax.broadcasted_iota(jnp.int32, (side, side), 1)
    left = lax.broadcasted_iota(jnp.int32, (8, side), 1) < half
    flat = scratch

    def one_piece(p, carry):
        high, low = split_pair(image_ref[p])
        first = jnp.dot(high, columns_ref[...], preferred_element_type=jnp.float32)
        second = jnp.dot(low, columns_ref[:, : KERNELS * side], preferred_element_type=jnp.float32)
        across = first[:, : KERNELS * side] + (first[:, KERNELS * side :] + second)
        matched = None
        for k in range(KERNELS):
            part = jnp.concatenate(split_pair(across[:, k * side : (k + 1) * side]), axis=1)
            both = jnp.dot(rows_ref[k], part, preferred_element_type=jnp.float32)
            smooth = both[:side, :side] + (both[:side, side:] + both[side:, :side])
            term = coeff_ref[p, k].astype(jnp.float32) * smooth
            matched = term if matched is None else matched + term
        piece = group * GROUP + p
        masked = (row_index == lines[0, piece]) | (lane_index == lines[1, piece])
        weight = jnp.where(masked, 0.0, inverse_ref[p])
        for plane, values in enumerate((weight * matched, weight)):
            for v in range(half // 8):
                upper = values[8 * v : 8 * v + 8]
                lower = values[half + 8 * v : half + 8 * v + 8]
                swapped_lower = pltpu.roll(lower, half, 1)
                swapped_upper = pltpu.roll(upper, half, 1)
                start = 8 * v * 32 + plane * 8 + p
                flat[pl.ds(start, 8, stride=32), :] = jnp.where(left, upper, swapped_lower)
                flat[pl.ds(start + 16, 8, stride=32), :] = jnp.where(left, swapped_upper, lower)
        return carry

    lax.fori_loop(0, GROUP, one_piece, 0, unroll=8)
    out_ref[...] = flat[...].reshape(out_ref.shape)


def match_pieces(images, coeffs, inverse_var, lines, slabs):
    pieces, wide = images.shape[0], images.shape[-1]
    side = inverse_var.shape[-1]
    columns, rows = kernel_bands(side, (wide - side) // 2)
    return pl.pallas_call(
        match_body,
        grid_spec=pltpu.PrefetchScalarGridSpec(
            num_scalar_prefetch=1,
            grid=(pieces // GROUP,),
            in_specs=[
                pl.BlockSpec((GROUP, wide, wide), lambda g, s: (g, 0, 0)),
                pl.BlockSpec((GROUP, KERNELS, side, side), lambda g, s: (g, 0, 0, 0)),
                pl.BlockSpec((GROUP, side, side), lambda g, s: (g, 0, 0)),
                pl.BlockSpec(columns.shape, lambda g, s: (0, 0)),
                pl.BlockSpec(rows.shape, lambda g, s: (0, 0, 0)),
            ],
            out_specs=pl.BlockSpec((slabs, 2 * GROUP, LANES), lambda g, s: (0, g, 0)),
            scratch_shapes=[pltpu.VMEM((slabs * 2 * GROUP, LANES), jnp.float32)],
        ),
        out_shape=jax.ShapeDtypeStruct((slabs, 2 * pieces, LANES), jnp.float32),
        compiler_params=pltpu.CompilerParams(vmem_limit_bytes=VMEM_LIMIT),
        name="match_pieces",
    )(lines, images, coeffs, inverse_var, jnp.asarray(columns), jnp.asarray(rows))


def sum_body(codes_ref, slab_ref, out_ref, total_ref):
    band = pl.program_id(0)
    holders, depth, lanes = slab_ref.shape
    patches = out_ref.shape[0] // pl.num_programs(0)
    pieces = holders * depth // 2
    both = slab_ref[...].reshape(holders * depth // (2 * GROUP), 2 * GROUP, lanes)
    values = jnp.concatenate(
        [both[:, :GROUP].reshape(pieces, lanes), both[:, GROUP:].reshape(pieces, lanes)], axis=1
    )
    high, low = split_pair(values)
    bins = lax.broadcasted_iota(jnp.int32, (patches * TILES, lanes), 0)
    joined = holders * lanes // pieces
    chosen = []
    for row in range(0, holders, joined):
        code = jnp.sum(codes_ref[0, row : row + joined, :], axis=0, keepdims=True)
        chosen.append(jnp.where(bins == code, 1.0, 0.0).astype(jnp.bfloat16))
    chosen = jnp.concatenate(chosen, axis=1)
    sums = jnp.dot(chosen, high, preferred_element_type=jnp.float32) + jnp.dot(
        chosen, low, preferred_element_type=jnp.float32
    )
    numerator, denominator = sums[:, :lanes], sums[:, lanes:]
    coadd = numerator / jnp.maximum(denominator, FLOOR)
    out_ref[pl.ds(band * patches, patches), :TILES, :] = coadd.reshape(patches, TILES, lanes)
    term = numerator * coadd

    @pl.when(band == 0)
    def _():
        total_ref[...] = term

    @pl.when(band > 0)
    def _():
        total_ref[...] += term

    @pl.when(band == pl.num_programs(0) - 1)
    def _():
        total = total_ref[...].reshape(patches, TILES_Y, TILES_X, lanes)
        for target in range(4):
            out_ref[target * patches : (target + 1) * patches, TILES:, :] = total[:, target // 2]


def sum_slabs(codes, slabs, bands, patches):
    devices, depth, lanes = slabs.shape
    rows = TILES + TILES_X
    return pl.pallas_call(
        sum_body,
        grid=(bands,),
        in_specs=[
            pl.BlockSpec((1, *codes.shape[1:]), lambda b: (b, 0, 0)),
            pl.BlockSpec((devices // bands, depth, lanes), lambda b: (b, 0, 0)),
        ],
        out_specs=pl.BlockSpec((devices, rows, lanes), lambda b: (0, 0, 0)),
        out_shape=jax.ShapeDtypeStruct((devices, rows, lanes), jnp.float32),
        scratch_shapes=[pltpu.VMEM((patches * TILES, lanes), jnp.float32)],
        compiler_params=pltpu.CompilerParams(vmem_limit_bytes=VMEM_LIMIT),
        name="sum_slabs",
    )(codes, slabs)


def place_body(which, part_ref, coadd_ref, detection_ref):
    lanes = part_ref.shape[-1]
    half = lanes // 2
    rows = TILES + TILES_X
    left = lax.broadcasted_iota(jnp.int32, (8, lanes), 1) < half
    for row in range(0, coadd_ref.shape[1], 8):
        for tile in range(rows):
            even = part_ref[pl.ds(2 * row * rows + tile, 8, stride=2 * rows), :]
            odd = part_ref[pl.ds((2 * row + 1) * rows + tile, 8, stride=2 * rows), :]
            upper = jnp.where(left, even, pltpu.roll(odd, half, 1))
            lower = jnp.where(left, pltpu.roll(even, half, 1), odd)
            column = (tile % TILES_X) * lanes
            if tile < TILES:
                top = 2 * (tile // TILES_X)
                coadd_ref[top, row : row + 8, column : column + lanes] = upper
                coadd_ref[top + 1, row : row + 8, column : column + lanes] = lower
            else:
                detection_ref[row : row + 8, column : column + lanes] = jnp.where(
                    which[0] == 0, upper, lower
                )


def place_parts(which, parts, side):
    devices, rows, lanes = parts.shape
    steps = 4
    half = side // 2
    return pl.pallas_call(
        place_body,
        grid_spec=pltpu.PrefetchScalarGridSpec(
            num_scalar_prefetch=1,
            grid=(steps,),
            in_specs=[pl.BlockSpec((devices * rows // steps, lanes), lambda g, s: (g, 0))],
            out_specs=[
                pl.BlockSpec((2 * TILES_Y, half // steps, TILES_X * lanes), lambda g, s: (0, g, 0)),
                pl.BlockSpec((half // steps, TILES_X * lanes), lambda g, s: (g, 0)),
            ],
        ),
        out_shape=[
            jax.ShapeDtypeStruct((2 * TILES_Y, half, TILES_X * lanes), jnp.float32),
            jax.ShapeDtypeStruct((half, TILES_X * lanes), jnp.float32),
        ],
        compiler_params=pltpu.CompilerParams(vmem_limit_bytes=PLACE_LIMIT),
        name="place_parts",
    )(which, parts.reshape(devices * rows, lanes))


def per_device(images, coeffs, inverse_var, bad_lines, destinations, tile_slots):
    bands, patches = lax.axis_size("band"), lax.axis_size("patch")
    side = inverse_var.shape[-1]
    code = destinations[0, :, 0] * TILES + tile_slots[0]
    pieces = code.shape[0]
    here = (jnp.arange(LANES) // pieces) == lax.axis_index("patch") % (LANES // pieces)
    code = jnp.where(here, jnp.tile(code, LANES // pieces), 0)
    code = jnp.broadcast_to(code, (bands * patches, 1, LANES))
    codes = lax.all_to_all(code, EVERY, split_axis=0, concat_axis=0, tiled=True)
    slabs = match_pieces(images[0], coeffs[0], inverse_var[0], bad_lines[0].T, bands * patches)
    slabs = lax.all_to_all(slabs, EVERY, split_axis=0, concat_axis=0, tiled=True)
    parts = sum_slabs(codes.reshape(bands, patches, LANES), slabs, bands, patches)
    parts = lax.all_to_all(parts, EVERY, split_axis=0, concat_axis=0, tiled=True)
    which = jnp.full((1,), lax.axis_index("band") % 2, jnp.int32)
    coadd, detection = place_parts(which, parts, side)
    return (coadd.reshape(1, 1, TILES_Y * side, TILES_X * side), detection[None])


def solution(mesh):
    in_specs = (
        P("band", "patch", None, None),
        P("band", "patch", None, None, None),
        P("band", "patch", None, None),
        P("band", "patch", None),
        P("band", "patch", None),
        P("band", "patch"),
    )
    out_specs = (P("band", "patch", None, None), P("patch", "band", None))
    return jax.shard_map(
        per_device, mesh=mesh, in_specs=in_specs, out_specs=out_specs, check_vma=False
    )
```

```python
import functools

import jax
import jax.numpy as jnp
import ml_dtypes
import numpy as np
from jax import lax
from jax.experimental import pallas as pl
from jax.experimental.pallas import tpu as pltpu
from jax.sharding import PartitionSpec as P

TILES_X = 8
TILES_Y = 2
TILES = TILES_X * TILES_Y
FRACTIONS = (0.12, 0.25, 0.45)
KERNELS = len(FRACTIONS)
FLOOR = 0.5
EVERY = ("band", "patch")
GROUP = 4
LANES = 128
VMEM_LIMIT = 60 << 20
SMALL_LIMIT = 24 << 20


def split_pair(values):
    high = values.astype(jnp.bfloat16)
    low = (values - high.astype(jnp.float32)).astype(jnp.bfloat16)
    return high, low


def kernel_bands(side, taps):
    offset = np.arange(side + 2 * taps)[None, :] - np.arange(side)[:, None]
    inside = (offset >= 0) & (offset <= 2 * taps)
    reach = np.arange(2 * taps + 1) - taps
    stacked = []
    for fraction in FRACTIONS:
        width = fraction * taps
        total = np.exp(-0.5 * (reach / width) ** 2).sum()
        full = np.where(inside, np.exp(-0.5 * ((offset - taps) / width) ** 2) / total, 0.0)
        full = full.astype(np.float32)
        high = full.astype(ml_dtypes.bfloat16)
        low = (full - high.astype(np.float32)).astype(ml_dtypes.bfloat16)
        stacked.append(np.concatenate([high, low, high], axis=1))
    columns = np.concatenate([matrix.T for matrix in stacked], axis=1)
    rows = np.stack(stacked)
    return columns, rows


def cut_rows(flat, values, start, step):
    side = values.shape[-1]
    half = side // 2
    left = lax.broadcasted_iota(jnp.int32, (8, side), 1) < half
    for row in range(0, half, 8):
        upper = values[row : row + 8]
        lower = values[half + row : half + row + 8]
        first = jnp.where(left, upper, pltpu.roll(lower, half, 1))
        second = jnp.where(left, pltpu.roll(upper, half, 1), lower)
        flat[pl.ds(start + 2 * row * step, 8, stride=2 * step), :] = first
        flat[pl.ds(start + (2 * row + 1) * step, 8, stride=2 * step), :] = second


def weight_of(lines, inverse, piece):
    row_index = lax.broadcasted_iota(jnp.int32, inverse.shape, 0)
    lane_index = lax.broadcasted_iota(jnp.int32, inverse.shape, 1)
    masked = (row_index == lines[0, piece]) | (lane_index == lines[1, piece])
    return jnp.where(masked, 0.0, inverse)


def match_body(lines, code_ref, image_ref, coeff_ref, inverse_ref, columns_ref, rows_ref, out_ref, *, depth):
    side = inverse_ref.shape[-1]
    group = pl.program_id(0)
    pieces = depth // 2

    @pl.when(group == 0)
    def _():
        code = jnp.broadcast_to(code_ref[...], (8, code_ref.shape[-1]))
        for slab in range(0, out_ref.shape[0] // depth, 8):
            out_ref[pl.ds(slab * depth + depth - 1, 8, stride=depth), :] = code

    def one_pair(pair, carry):
        across = []
        for p in (2 * pair, 2 * pair + 1):
            high, low = split_pair(image_ref[p])
            stacked = jnp.concatenate([high, high, low], axis=1)
            across.append(jnp.dot(stacked, columns_ref[...], preferred_element_type=jnp.float32))
        matched = None
        for k in range(KERNELS):
            both = jnp.concatenate([part[:, k * side : (k + 1) * side] for part in across], axis=1)
            high = both.astype(jnp.bfloat16).astype(jnp.float32)
            stacked = jnp.concatenate([high, high, both - high], axis=0).astype(jnp.bfloat16)
            smooth = jnp.dot(rows_ref[k], stacked, preferred_element_type=jnp.float32)
            terms = [
                coeff_ref[2 * pair + n, k].astype(jnp.float32) * smooth[:, n * side : (n + 1) * side]
                for n in range(2)
            ]
            matched = terms if matched is None else [a + b for a, b in zip(matched, terms)]
        for n in range(2):
            p = 2 * pair + n
            piece = group * GROUP + p
            weight = weight_of(lines, inverse_ref[p], piece)
            cut_rows(out_ref, weight * matched[n], piece, depth)
            cut_rows(out_ref, weight, pieces + piece, depth)
        return carry

    lax.fori_loop(0, GROUP // 2, one_pair, 0, unroll=True)


def match_pieces(images, coeffs, inverse_var, lines, code, slabs):
    pieces, wide = images.shape[0], images.shape[-1]
    side = inverse_var.shape[-1]
    depth = 2 * pieces + 1
    columns, rows = kernel_bands(side, (wide - side) // 2)
    return pl.pallas_call(
        functools.partial(match_body, depth=depth),
        grid_spec=pltpu.PrefetchScalarGridSpec(
            num_scalar_prefetch=1,
            grid=(pieces // GROUP,),
            in_specs=[
                pl.BlockSpec((1, LANES), lambda g, s: (0, 0)),
                pl.BlockSpec((GROUP, wide, wide), lambda g, s: (g, 0, 0)),
                pl.BlockSpec((GROUP, KERNELS, side, side), lambda g, s: (g, 0, 0, 0)),
                pl.BlockSpec((GROUP, side, side), lambda g, s: (g, 0, 0)),
                pl.BlockSpec(columns.shape, lambda g, s: (0, 0)),
                pl.BlockSpec(rows.shape, lambda g, s: (0, 0, 0)),
            ],
            out_specs=pl.BlockSpec((slabs * depth, LANES), lambda g, s: (0, 0)),
        ),
        out_shape=jax.ShapeDtypeStruct((slabs * depth, LANES), jnp.float32),
        compiler_params=pltpu.CompilerParams(vmem_limit_bytes=VMEM_LIMIT),
        name="match_pieces",
    )(lines, code, images, coeffs, inverse_var, jnp.asarray(columns), jnp.asarray(rows))


def binned_sum(chosen, values):
    lanes = values.shape[-1]
    pair = jnp.concatenate(split_pair(values), axis=1)
    sums = jnp.dot(chosen, pair, preferred_element_type=jnp.float32)
    return sums[:, :lanes] + sums[:, lanes:]


def sum_body(slab_ref, out_ref, total_ref, *, depth):
    band, bands = pl.program_id(0), pl.num_programs(0)
    lanes = slab_ref.shape[-1]
    pieces = depth // 2
    holders = slab_ref.shape[0] // depth
    joined = lanes // pieces
    bins_count = total_ref.shape[0]
    patches = bins_count // TILES
    def plane(first):
        return jnp.concatenate(
            [slab_ref[pl.ds(s * depth + first + m, 8), :] for s in range(holders) for m in range(0, pieces, 8)]
        )

    bins = lax.broadcasted_iota(jnp.int32, (bins_count, lanes), 0)
    chosen = []
    for first in range(0, holders, joined):
        code = slab_ref[pl.ds(first * depth + depth - 1, 1), :]
        for s in range(first + 1, first + joined):
            code = code + slab_ref[pl.ds(s * depth + depth - 1, 1), :]
        chosen.append(jnp.where(bins == code.astype(jnp.int32), 1.0, 0.0).astype(jnp.bfloat16))
    chosen = jnp.concatenate(chosen, axis=1)
    numerator = binned_sum(chosen, plane(0))
    denominator = binned_sum(chosen, plane(pieces))
    coadd = numerator / jnp.maximum(denominator, FLOOR)
    out_ref[pl.ds(band * patches, patches), :TILES, :] = coadd.reshape(patches, TILES, lanes)
    term = numerator * coadd

    @pl.when(band == 0)
    def _():
        total_ref[...] = term

    @pl.when(band > 0)
    def _():
        total_ref[...] += term

    @pl.when(band == bands - 1)
    def _():
        total = total_ref[...].reshape(patches, TILES_Y, TILES_X, lanes)
        for target in range(4):
            out_ref[target * patches : (target + 1) * patches, TILES:, :] = total[:, target // 2]


def sum_slabs(slabs, bands, patches, depth):
    devices, lanes = bands * patches, slabs.shape[-1]
    rows = TILES + TILES_X
    return pl.pallas_call(
        functools.partial(sum_body, depth=depth),
        grid=(bands,),
        in_specs=[pl.BlockSpec((slabs.shape[0] // bands, lanes), lambda b: (b, 0))],
        out_specs=pl.BlockSpec((devices, rows, lanes), lambda b: (0, 0, 0)),
        out_shape=jax.ShapeDtypeStruct((devices, rows, lanes), jnp.float32),
        scratch_shapes=[pltpu.VMEM((patches * TILES, lanes), jnp.float32)],
        compiler_params=pltpu.CompilerParams(vmem_limit_bytes=SMALL_LIMIT),
        name="sum_slabs",
    )(slabs)


def place_body(which, part_ref, coadd_ref, detection_ref):
    lanes = part_ref.shape[-1]
    half = lanes // 2
    rows = TILES + TILES_X
    left = lax.broadcasted_iota(jnp.int32, (8, lanes), 1) < half
    for row in range(0, coadd_ref.shape[1], 8):
        for tile in range(rows):
            even = part_ref[pl.ds(2 * row * rows + tile, 8, stride=2 * rows), :]
            odd = part_ref[pl.ds((2 * row + 1) * rows + tile, 8, stride=2 * rows), :]
            upper = jnp.where(left, even, pltpu.roll(odd, half, 1))
            lower = jnp.where(left, pltpu.roll(even, half, 1), odd)
            column = (tile % TILES_X) * lanes
            if tile < TILES:
                top = 2 * (tile // TILES_X)
                coadd_ref[top, row : row + 8, column : column + lanes] = upper
                coadd_ref[top + 1, row : row + 8, column : column + lanes] = lower
            else:
                detection_ref[row : row + 8, column : column + lanes] = jnp.where(
                    which[0] == 0, upper, lower
                )


def place_parts(which, parts, side):
    devices, rows, lanes = parts.shape
    steps = 4
    half = side // 2
    return pl.pallas_call(
        place_body,
        grid_spec=pltpu.PrefetchScalarGridSpec(
            num_scalar_prefetch=1,
            grid=(steps,),
            in_specs=[pl.BlockSpec((devices * rows // steps, lanes), lambda g, s: (g, 0))],
            out_specs=[
                pl.BlockSpec((2 * TILES_Y, half // steps, TILES_X * lanes), lambda g, s: (0, g, 0)),
                pl.BlockSpec((half // steps, TILES_X * lanes), lambda g, s: (g, 0)),
            ],
        ),
        out_shape=[
            jax.ShapeDtypeStruct((2 * TILES_Y, half, TILES_X * lanes), jnp.float32),
            jax.ShapeDtypeStruct((half, TILES_X * lanes), jnp.float32),
        ],
        compiler_params=pltpu.CompilerParams(vmem_limit_bytes=SMALL_LIMIT),
        name="place_parts",
    )(which, parts.reshape(devices * rows, lanes))


def exchange(rows, devices):
    lanes = rows.shape[-1]
    chunks = rows.reshape(devices, -1, 1, lanes)
    return lax.all_to_all(chunks, EVERY, split_axis=0, concat_axis=0, tiled=True).reshape(-1, lanes)


def per_device(images, coeffs, inverse_var, bad_lines, destinations, tile_slots):
    bands, patches = lax.axis_size("band"), lax.axis_size("patch")
    devices = bands * patches
    pieces, side = inverse_var.shape[1:3]
    lines = bad_lines[0].T
    code = (destinations[0, :, 0] * TILES + tile_slots[0]).astype(jnp.float32)
    here = (jnp.arange(LANES) // pieces) == lax.axis_index("patch") % (LANES // pieces)
    code = jnp.where(here, jnp.tile(code, LANES // pieces), 0.0)[None]
    slabs = match_pieces(images[0], coeffs[0], inverse_var[0], lines, code, devices)
    slabs = exchange(slabs, devices)
    parts = sum_slabs(slabs, bands, patches, 2 * pieces + 1)
    parts = lax.all_to_all(parts, EVERY, split_axis=0, concat_axis=0, tiled=True)
    which = jnp.full((1,), lax.axis_index("band") % 2, jnp.int32)
    coadd, detection = place_parts(which, parts, side)
    return (coadd.reshape(1, 1, TILES_Y * side, TILES_X * side), detection[None])


def solution(mesh):
    in_specs = (
        P("band", "patch", None, None),
        P("band", "patch", None, None, None),
        P("band", "patch", None, None),
        P("band", "patch", None),
        P("band", "patch", None),
        P("band", "patch"),
    )
    out_specs = (P("band", "patch", None, None), P("patch", "band", None))
    return jax.shard_map(
        per_device, mesh=mesh, in_specs=in_specs, out_specs=out_specs, check_vma=False
    )
```

```python
import functools

import jax
import jax.numpy as jnp
import ml_dtypes
import numpy as np
from jax import lax
from jax.experimental import pallas as pl
from jax.experimental.pallas import tpu as pltpu
from jax.sharding import PartitionSpec as P

TILES_X = 8
TILES_Y = 2
TILES = TILES_X * TILES_Y
FRACTIONS = (0.12, 0.25, 0.45)
KERNELS = len(FRACTIONS)
FLOOR = 0.5
EVERY = ("band", "patch")
GROUP = 8
PART_ROWS = TILES + TILES_X // 2
LANES = 128
VMEM_LIMIT = 40 << 20
SMALL_LIMIT = 24 << 20


def split_pair(values):
    high = values.astype(jnp.bfloat16)
    low = (values - high.astype(jnp.float32)).astype(jnp.bfloat16)
    return high, low


def kernel_bands(side, taps):
    offset = np.arange(side + 2 * taps)[None, :] - np.arange(side)[:, None]
    inside = (offset >= 0) & (offset <= 2 * taps)
    reach = np.arange(2 * taps + 1) - taps
    stacked = []
    for fraction in FRACTIONS:
        width = fraction * taps
        total = np.exp(-0.5 * (reach / width) ** 2).sum()
        full = np.where(inside, np.exp(-0.5 * ((offset - taps) / width) ** 2) / total, 0.0)
        full = full.astype(np.float32)
        high = full.astype(ml_dtypes.bfloat16)
        low = (full - high.astype(np.float32)).astype(ml_dtypes.bfloat16)
        stacked.append(np.concatenate([high, low, high], axis=1))
    columns = np.concatenate([matrix.T for matrix in stacked], axis=1)
    rows = np.stack(stacked)
    return columns, rows


def cut_rows(flat, values, start, step):
    side = values.shape[-1]
    half = side // 2
    left = lax.broadcasted_iota(jnp.int32, (8, side), 1) < half
    for row in range(0, half, 8):
        upper = values[row : row + 8]
        lower = values[half + row : half + row + 8]
        first = jnp.where(left, upper, pltpu.roll(lower, half, 1))
        second = jnp.where(left, pltpu.roll(upper, half, 1), lower)
        flat[pl.ds(start + 2 * row * step, 8, stride=2 * step), :] = first
        flat[pl.ds(start + (2 * row + 1) * step, 8, stride=2 * step), :] = second


def weight_of(lines, inverse, piece):
    row_index = lax.broadcasted_iota(jnp.int32, inverse.shape, 0)
    lane_index = lax.broadcasted_iota(jnp.int32, inverse.shape, 1)
    masked = (row_index == lines[0, piece]) | (lane_index == lines[1, piece])
    return jnp.where(masked, 0.0, inverse)


def match_body(
    lines, place, owner_ref, tile_ref, image_ref, coeff_ref, inverse_ref, columns_ref, rows_ref, out_ref, *, depth
):
    side = inverse_ref.shape[-1]
    group = pl.program_id(0)
    pieces = depth // 2

    @pl.when(group == 0)
    def _():
        code = (owner_ref[...] * TILES + tile_ref[...]).astype(jnp.float32)
        code = jnp.concatenate([code] * (LANES // pieces), axis=1)
        part = lax.broadcasted_iota(jnp.int32, code.shape, 1) // pieces
        code = jnp.where(part == lax.rem(place[0], LANES // pieces), code, 0.0)
        code = jnp.broadcast_to(code, (8, LANES))
        for slab in range(0, out_ref.shape[0] // depth, 8):
            out_ref[pl.ds(slab * depth + depth - 1, 8, stride=depth), :] = code

    high, low = split_pair(image_ref[...].reshape(-1, image_ref.shape[-1]))
    stacked = jnp.concatenate([high, high, low], axis=1)
    across_all = jnp.dot(stacked, columns_ref[...], preferred_element_type=jnp.float32)

    def one_pair(pair, carry):
        wide = image_ref.shape[-1]
        across = [across_all[(2 * pair + n) * wide : (2 * pair + n + 1) * wide] for n in range(2)]
        matched = None
        for k in range(KERNELS):
            both = jnp.concatenate([part[:, k * side : (k + 1) * side] for part in across], axis=1)
            high = both.astype(jnp.bfloat16).astype(jnp.float32)
            stacked = jnp.concatenate([high, high, both - high], axis=0).astype(jnp.bfloat16)
            smooth = jnp.dot(rows_ref[k], stacked, preferred_element_type=jnp.float32)
            terms = [
                coeff_ref[2 * pair + n, k].astype(jnp.float32) * smooth[:, n * side : (n + 1) * side]
                for n in range(2)
            ]
            matched = terms if matched is None else [a + b for a, b in zip(matched, terms)]
        for n in range(2):
            p = 2 * pair + n
            piece = group * GROUP + p
            weight = weight_of(lines, inverse_ref[p], piece)
            cut_rows(out_ref, weight * matched[n], piece, depth)
            cut_rows(out_ref, weight, pieces + piece, depth)
        return carry

    for pair in range(GROUP // 2):
        one_pair(pair, 0)


def match_pieces(images, coeffs, inverse_var, lines, place, owners, tiles, slabs):
    pieces, wide = images.shape[0], images.shape[-1]
    side = inverse_var.shape[-1]
    depth = 2 * pieces + 1
    columns, rows = kernel_bands(side, (wide - side) // 2)
    kept = (lines, place, owners, tiles, images, coeffs, inverse_var, jnp.asarray(columns), jnp.asarray(rows))
    kept = [pltpu.with_memory_space_constraint(array, pltpu.HBM) for array in kept]
    return pl.pallas_call(
        functools.partial(match_body, depth=depth),
        grid_spec=pltpu.PrefetchScalarGridSpec(
            num_scalar_prefetch=2,
            grid=(pieces // GROUP,),
            in_specs=[
                pl.BlockSpec((1, pieces), lambda g, *_: (0, 0)),
                pl.BlockSpec((1, pieces), lambda g, *_: (0, 0)),
                pl.BlockSpec((GROUP, wide, wide), lambda g, *_: (g, 0, 0)),
                pl.BlockSpec((GROUP, KERNELS, side, side), lambda g, *_: (g, 0, 0, 0)),
                pl.BlockSpec((GROUP, side, side), lambda g, *_: (g, 0, 0)),
                pl.BlockSpec(columns.shape, lambda g, *_: (0, 0)),
                pl.BlockSpec(rows.shape, lambda g, *_: (0, 0, 0)),
            ],
            out_specs=pl.BlockSpec((slabs * depth, LANES), lambda g, *_: (0, 0)),
        ),
        out_shape=jax.ShapeDtypeStruct((slabs * depth, LANES), jnp.float32),
        compiler_params=pltpu.CompilerParams(vmem_limit_bytes=VMEM_LIMIT),
        name="match_pieces",
    )(*kept)


def binned_sum(chosen, values):
    lanes = values.shape[-1]
    pair = jnp.concatenate(split_pair(values), axis=1)
    sums = jnp.dot(chosen, pair, preferred_element_type=jnp.float32)
    return sums[:, :lanes] + sums[:, lanes:]


def sum_body(slab_ref, out_ref, *, depth, bands):
    lanes = slab_ref.shape[-1]
    half = lanes // 2
    pieces = depth // 2
    holders = slab_ref.shape[0] // (depth * bands)
    joined = lanes // pieces
    patches = out_ref.shape[0] // (PART_ROWS * bands)
    bins = lax.broadcasted_iota(jnp.int32, (patches * TILES, lanes), 0)
    total = None
    for band in range(bands):
        starts = [(band * holders + s) * depth for s in range(holders)]

        def plane(first):
            return jnp.concatenate(
                [slab_ref[start + first + m : start + first + m + 8, :] for start in starts for m in range(0, pieces, 8)]
            )

        chosen = []
        for first in range(0, holders, joined):
            code = sum(slab_ref[start + depth - 1 : start + depth, :] for start in starts[first : first + joined])
            chosen.append(jnp.where(bins == code.astype(jnp.int32), 1.0, 0.0).astype(jnp.bfloat16))
        chosen = jnp.concatenate(chosen, axis=1)
        numerator = binned_sum(chosen, plane(0))
        denominator = binned_sum(chosen, plane(pieces))
        coadd = numerator / jnp.maximum(denominator, FLOOR)
        for patch in range(patches):
            start = (band * patches + patch) * PART_ROWS
            out_ref[start : start + TILES, :] = coadd[patch * TILES : (patch + 1) * TILES]
        term = numerator * coadd
        total = term if total is None else total + term
    left = lax.broadcasted_iota(jnp.int32, (TILES_X, lanes), 1) < half
    for patch in range(patches):
        for top in range(TILES_Y):
            first = (patch * TILES_Y + top) * TILES_X
            tiles = total[first : first + TILES_X]
            later = pltpu.roll(tiles, TILES_X // 2, 0)
            upper = jnp.where(left, tiles, pltpu.roll(later, half, 1))
            lower = jnp.where(left, pltpu.roll(tiles, half, 1), later)
            for low, packed in enumerate((upper, lower)):
                start = ((2 * top + low) * patches + patch) * PART_ROWS + TILES
                out_ref[start : start + TILES_X // 2, :] = packed[: TILES_X // 2]


def sum_slabs(slabs, bands, patches, depth):
    rows, lanes = bands * patches * PART_ROWS, slabs.shape[-1]
    return pl.pallas_call(
        functools.partial(sum_body, depth=depth, bands=bands),
        in_specs=[pl.BlockSpec(memory_space=pltpu.VMEM)],
        out_specs=pl.BlockSpec(memory_space=pltpu.VMEM),
        out_shape=jax.ShapeDtypeStruct((rows, lanes), jnp.float32),
        compiler_params=pltpu.CompilerParams(vmem_limit_bytes=SMALL_LIMIT),
        name="sum_slabs",
    )(slabs)


def place_body(part_ref, coadd_ref, detection_ref):
    lanes = part_ref.shape[-1]
    half = lanes // 2
    left = lax.broadcasted_iota(jnp.int32, (8, lanes), 1) < half

    def column(tile):
        return pl.ds(tile % TILES_X * lanes, lanes)

    for row in range(0, coadd_ref.shape[1], 8):
        for part in range(PART_ROWS):
            even = part_ref[pl.ds(2 * row * PART_ROWS + part, 8, stride=2 * PART_ROWS), :]
            odd = part_ref[pl.ds((2 * row + 1) * PART_ROWS + part, 8, stride=2 * PART_ROWS), :]
            first = jnp.where(left, even, pltpu.roll(odd, half, 1))
            second = jnp.where(left, pltpu.roll(even, half, 1), odd)
            if part < TILES:
                top = 2 * (part // TILES_X)
                coadd_ref[top, row : row + 8, column(part)] = first
                coadd_ref[top + 1, row : row + 8, column(part)] = second
            else:
                detection_ref[row : row + 8, column(part - TILES)] = first
                detection_ref[row : row + 8, column(part - TILES + TILES_X // 2)] = second


def place_parts(parts, side):
    rows, lanes = parts.shape
    steps = 4
    half = side // 2
    return pl.pallas_call(
        place_body,
        grid=(steps,),
        in_specs=[pl.BlockSpec((rows // steps, lanes), lambda g: (g, 0))],
        out_specs=[
            pl.BlockSpec((2 * TILES_Y, half // steps, TILES_X * lanes), lambda g: (0, g, 0)),
            pl.BlockSpec((half // steps, TILES_X * lanes), lambda g: (g, 0)),
        ],
        out_shape=[
            jax.ShapeDtypeStruct((2 * TILES_Y, half, TILES_X * lanes), jnp.float32),
            jax.ShapeDtypeStruct((half, TILES_X * lanes), jnp.float32),
        ],
        compiler_params=pltpu.CompilerParams(vmem_limit_bytes=SMALL_LIMIT),
        name="place_parts",
    )(parts)


def exchange(rows, devices):
    lanes = rows.shape[-1]
    chunks = rows.reshape(devices, -1, 1, lanes)
    return lax.all_to_all(chunks, EVERY, split_axis=0, concat_axis=0, tiled=True).reshape(-1, lanes)


def per_device(images, coeffs, inverse_var, bad_lines, destinations, tile_slots):
    bands, patches = lax.axis_size("band"), lax.axis_size("patch")
    devices = bands * patches
    pieces, side = inverse_var.shape[1:3]
    lines = bad_lines[0].T
    place = jnp.full((1,), lax.axis_index("patch"), jnp.int32)
    owners = destinations[:, :, 0]
    slabs = match_pieces(images[0], coeffs[0], inverse_var[0], lines, place, owners, tile_slots, devices)
    slabs = exchange(slabs, devices)
    parts = sum_slabs(slabs, bands, patches, 2 * pieces + 1)
    coadd, detection = place_parts(exchange(parts, devices), side)
    return (coadd.reshape(1, 1, TILES_Y * side, TILES_X * side), detection[None])


def solution(mesh):
    in_specs = (
        P("band", "patch", None, None),
        P("band", "patch", None, None, None),
        P("band", "patch", None, None),
        P("band", "patch", None),
        P("band", "patch", None),
        P("band", "patch"),
    )
    out_specs = (P("band", "patch", None, None), P("patch", "band", None))
    return jax.shard_map(
        per_device, mesh=mesh, in_specs=in_specs, out_specs=out_specs, check_vma=False
    )
```

```python
import functools

import jax
import jax.numpy as jnp
import ml_dtypes
import numpy as np
from jax import lax
from jax.experimental import pallas as pl
from jax.experimental.pallas import tpu as pltpu
from jax.sharding import PartitionSpec as P

TILES_X = 8
TILES_Y = 2
TILES = TILES_X * TILES_Y
FRACTIONS = (0.12, 0.25, 0.45)
KERNELS = len(FRACTIONS)
FLOOR = 0.5
EVERY = ("band", "patch")
GROUP = 8
PART_ROWS = TILES + TILES_X // 2
LANES = 128
VMEM_LIMIT = 40 << 20
SMALL_LIMIT = 24 << 20


def split_pair(values):
    high = values.astype(jnp.bfloat16)
    low = (values - high.astype(jnp.float32)).astype(jnp.bfloat16)
    return high, low


def kernel_bands(side, taps):
    offset = np.arange(side + 2 * taps)[None, :] - np.arange(side)[:, None]
    inside = (offset >= 0) & (offset <= 2 * taps)
    reach = np.arange(2 * taps + 1) - taps
    stacked = []
    for fraction in FRACTIONS:
        width = fraction * taps
        total = np.exp(-0.5 * (reach / width) ** 2).sum()
        full = np.where(inside, np.exp(-0.5 * ((offset - taps) / width) ** 2) / total, 0.0)
        full = full.astype(np.float32)
        high = full.astype(ml_dtypes.bfloat16)
        low = (full - high.astype(np.float32)).astype(ml_dtypes.bfloat16)
        stacked.append(np.concatenate([high, low, high], axis=1))
    columns = np.concatenate([matrix.T for matrix in stacked], axis=1)
    rows = np.stack(stacked)
    return columns, rows


def cut_rows(flat, values, start, step):
    side = values.shape[-1]
    half = side // 2
    left = lax.broadcasted_iota(jnp.int32, (8, side), 1) < half
    for row in range(0, half, 8):
        upper = values[row : row + 8]
        lower = values[half + row : half + row + 8]
        first = jnp.where(left, upper, pltpu.roll(lower, half, 1))
        second = jnp.where(left, pltpu.roll(upper, half, 1), lower)
        flat[pl.ds(start + 2 * row * step, 8, stride=2 * step), :] = first
        flat[pl.ds(start + (2 * row + 1) * step, 8, stride=2 * step), :] = second


def weight_of(lines, inverse, piece):
    row_index = lax.broadcasted_iota(jnp.int32, inverse.shape, 0)
    lane_index = lax.broadcasted_iota(jnp.int32, inverse.shape, 1)
    masked = (row_index == lines[0, piece]) | (lane_index == lines[1, piece])
    return jnp.where(masked, 0.0, inverse)


def match_body(
    lines, place, owner_ref, tile_ref, image_ref, coeff_ref, inverse_ref, columns_ref, rows_ref, out_ref, *, depth
):
    side = inverse_ref.shape[-1]
    group = pl.program_id(0)
    pieces = depth // 2

    @pl.when(group == 0)
    def _():
        code = (owner_ref[...] * TILES + tile_ref[...]).astype(jnp.float32)
        code = jnp.concatenate([code] * (LANES // pieces), axis=1)
        part = lax.broadcasted_iota(jnp.int32, code.shape, 1) // pieces
        code = jnp.where(part == lax.rem(place[0], LANES // pieces), code, 0.0)
        code = jnp.broadcast_to(code, (8, LANES))
        for slab in range(0, out_ref.shape[0] // depth, 8):
            out_ref[pl.ds(slab * depth + depth - 1, 8, stride=depth), :] = code

    high, low = split_pair(image_ref[...].reshape(-1, image_ref.shape[-1]))
    stacked = jnp.concatenate([high, high, low], axis=1)
    across_all = jnp.dot(stacked, columns_ref[...], preferred_element_type=jnp.float32)

    def one_pair(pair, carry):
        wide = image_ref.shape[-1]
        across = [across_all[(2 * pair + n) * wide : (2 * pair + n + 1) * wide] for n in range(2)]
        matched = None
        for k in range(KERNELS):
            both = jnp.concatenate([part[:, k * side : (k + 1) * side] for part in across], axis=1)
            high = both.astype(jnp.bfloat16).astype(jnp.float32)
            stacked = jnp.concatenate([high, high, both - high], axis=0).astype(jnp.bfloat16)
            smooth = jnp.dot(rows_ref[k], stacked, preferred_element_type=jnp.float32)
            terms = [
                coeff_ref[2 * pair + n, k].astype(jnp.float32) * smooth[:, n * side : (n + 1) * side]
                for n in range(2)
            ]
            matched = terms if matched is None else [a + b for a, b in zip(matched, terms)]
        for n in range(2):
            p = 2 * pair + n
            piece = group * GROUP + p
            weight = weight_of(lines, inverse_ref[p], piece)
            cut_rows(out_ref, weight * matched[n], piece, depth)
            cut_rows(out_ref, weight, pieces + piece, depth)
        return carry

    for pair in range(GROUP // 2):
        one_pair(pair, 0)


def match_pieces(images, coeffs, inverse_var, lines, place, owners, tiles, slabs):
    pieces, wide = images.shape[0], images.shape[-1]
    side = inverse_var.shape[-1]
    depth = 2 * pieces + 1
    columns, rows = kernel_bands(side, (wide - side) // 2)
    kept = (lines, place, owners, tiles, images, coeffs, inverse_var, jnp.asarray(columns), jnp.asarray(rows))
    kept = [pltpu.with_memory_space_constraint(array, pltpu.HBM) for array in kept]
    return pl.pallas_call(
        functools.partial(match_body, depth=depth),
        grid_spec=pltpu.PrefetchScalarGridSpec(
            num_scalar_prefetch=2,
            grid=(pieces // GROUP,),
            in_specs=[
                pl.BlockSpec((1, pieces), lambda g, *_: (0, 0)),
                pl.BlockSpec((1, pieces), lambda g, *_: (0, 0)),
                pl.BlockSpec((GROUP, wide, wide), lambda g, *_: (g, 0, 0)),
                pl.BlockSpec((GROUP, KERNELS, side, side), lambda g, *_: (g, 0, 0, 0)),
                pl.BlockSpec((GROUP, side, side), lambda g, *_: (g, 0, 0)),
                pl.BlockSpec(columns.shape, lambda g, *_: (0, 0)),
                pl.BlockSpec(rows.shape, lambda g, *_: (0, 0, 0)),
            ],
            out_specs=pl.BlockSpec((slabs * depth, LANES), lambda g, *_: (0, 0)),
        ),
        out_shape=jax.ShapeDtypeStruct((slabs * depth, LANES), jnp.float32),
        compiler_params=pltpu.CompilerParams(vmem_limit_bytes=VMEM_LIMIT),
        name="match_pieces",
    )(*kept)


def binned_sum(chosen, values):
    lanes = values.shape[-1]
    pair = jnp.concatenate(split_pair(values), axis=1)
    sums = jnp.dot(chosen, pair, preferred_element_type=jnp.float32)
    return sums[:, :lanes] + sums[:, lanes:]


def sum_body(slab_ref, out_ref, *, depth, bands):
    lanes = slab_ref.shape[-1]
    half = lanes // 2
    pieces = depth // 2
    holders = slab_ref.shape[0] // (depth * bands)
    joined = lanes // pieces
    patches = out_ref.shape[0] // (PART_ROWS * bands)
    bins = lax.broadcasted_iota(jnp.int32, (patches * TILES, lanes), 0)
    total = None
    for band in range(bands):
        starts = [(band * holders + s) * depth for s in range(holders)]

        def plane(first):
            return jnp.concatenate(
                [slab_ref[start + first + m : start + first + m + 8, :] for start in starts for m in range(0, pieces, 8)]
            )

        chosen = []
        for first in range(0, holders, joined):
            code = sum(slab_ref[start + depth - 1 : start + depth, :] for start in starts[first : first + joined])
            chosen.append(jnp.where(bins == code.astype(jnp.int32), 1.0, 0.0).astype(jnp.bfloat16))
        chosen = jnp.concatenate(chosen, axis=1)
        numerator = binned_sum(chosen, plane(0))
        denominator = binned_sum(chosen, plane(pieces))
        coadd = numerator / jnp.maximum(denominator, FLOOR)
        for patch in range(patches):
            start = (band * patches + patch) * PART_ROWS
            out_ref[start : start + TILES, :] = coadd[patch * TILES : (patch + 1) * TILES]
        term = numerator * coadd
        total = term if total is None else total + term
    left = lax.broadcasted_iota(jnp.int32, (TILES_X, lanes), 1) < half
    for patch in range(patches):
        for top in range(TILES_Y):
            first = (patch * TILES_Y + top) * TILES_X
            tiles = total[first : first + TILES_X]
            later = pltpu.roll(tiles, TILES_X // 2, 0)
            upper = jnp.where(left, tiles, pltpu.roll(later, half, 1))
            lower = jnp.where(left, pltpu.roll(tiles, half, 1), later)
            for low, packed in enumerate((upper, lower)):
                start = ((2 * top + low) * patches + patch) * PART_ROWS + TILES
                out_ref[start : start + TILES_X // 2, :] = packed[: TILES_X // 2]


def sum_slabs(slabs, bands, patches, depth):
    rows, lanes = bands * patches * PART_ROWS, slabs.shape[-1]
    return pl.pallas_call(
        functools.partial(sum_body, depth=depth, bands=bands),
        in_specs=[pl.BlockSpec(memory_space=pltpu.VMEM)],
        out_specs=pl.BlockSpec(memory_space=pltpu.VMEM),
        out_shape=jax.ShapeDtypeStruct((rows, lanes), jnp.float32),
        compiler_params=pltpu.CompilerParams(vmem_limit_bytes=SMALL_LIMIT),
        name="sum_slabs",
    )(slabs)


def place_body(part_ref, coadd_ref, detection_ref):
    lanes = part_ref.shape[-1]
    half = lanes // 2
    left = lax.broadcasted_iota(jnp.int32, (8, lanes), 1) < half

    def column(tile):
        return pl.ds(tile % TILES_X * lanes, lanes)

    base = pl.program_id(0) * 2 * coadd_ref.shape[1] * PART_ROWS
    for row in range(0, coadd_ref.shape[1], 8):
        for part in range(PART_ROWS):
            start = base + 2 * row * PART_ROWS + part
            even = part_ref[pl.ds(start, 8, stride=2 * PART_ROWS), :]
            odd = part_ref[pl.ds(start + PART_ROWS, 8, stride=2 * PART_ROWS), :]
            first = jnp.where(left, even, pltpu.roll(odd, half, 1))
            second = jnp.where(left, pltpu.roll(even, half, 1), odd)
            if part < TILES:
                top = 2 * (part // TILES_X)
                coadd_ref[top, row : row + 8, column(part)] = first
                coadd_ref[top + 1, row : row + 8, column(part)] = second
            else:
                detection_ref[row : row + 8, column(part - TILES)] = first
                detection_ref[row : row + 8, column(part - TILES + TILES_X // 2)] = second


def place_parts(parts, side):
    lanes = parts.shape[-1]
    steps = 4
    half = side // 2
    return pl.pallas_call(
        place_body,
        grid=(steps,),
        in_specs=[pl.BlockSpec(memory_space=pltpu.VMEM)],
        out_specs=[
            pl.BlockSpec((2 * TILES_Y, half // steps, TILES_X * lanes), lambda g: (0, g, 0)),
            pl.BlockSpec((half // steps, TILES_X * lanes), lambda g: (g, 0)),
        ],
        out_shape=[
            jax.ShapeDtypeStruct((2 * TILES_Y, half, TILES_X * lanes), jnp.float32),
            jax.ShapeDtypeStruct((half, TILES_X * lanes), jnp.float32),
        ],
        compiler_params=pltpu.CompilerParams(vmem_limit_bytes=SMALL_LIMIT),
        name="place_parts",
    )(parts)


def exchange(rows, devices):
    lanes = rows.shape[-1]
    chunks = rows.reshape(devices, -1, 1, lanes)
    return lax.all_to_all(chunks, EVERY, split_axis=0, concat_axis=0, tiled=True).reshape(-1, lanes)


def per_device(images, coeffs, inverse_var, bad_lines, destinations, tile_slots):
    bands, patches = lax.axis_size("band"), lax.axis_size("patch")
    devices = bands * patches
    pieces, side = inverse_var.shape[1:3]
    lines = bad_lines[0].T
    place = jnp.full((1,), lax.axis_index("patch"), jnp.int32)
    owners = destinations[:, :, 0]
    slabs = match_pieces(images[0], coeffs[0], inverse_var[0], lines, place, owners, tile_slots, devices)
    slabs = exchange(slabs, devices)
    parts = sum_slabs(slabs, bands, patches, 2 * pieces + 1)
    coadd, detection = place_parts(exchange(parts, devices), side)
    return (coadd.reshape(1, 1, TILES_Y * side, TILES_X * side), detection[None])


def solution(mesh):
    in_specs = (
        P("band", "patch", None, None),
        P("band", "patch", None, None, None),
        P("band", "patch", None, None),
        P("band", "patch", None),
        P("band", "patch", None),
        P("band", "patch"),
    )
    out_specs = (P("band", "patch", None, None), P("patch", "band", None))
    return jax.shard_map(
        per_device, mesh=mesh, in_specs=in_specs, out_specs=out_specs, check_vma=False
    )
```

```python
import functools

import jax
import jax.numpy as jnp
import ml_dtypes
import numpy as np
from jax import lax
from jax.experimental import pallas as pl
from jax.experimental.pallas import tpu as pltpu
from jax.sharding import PartitionSpec as P

TILES_X = 8
TILES_Y = 2
TILES = TILES_X * TILES_Y
FRACTIONS = (0.12, 0.25, 0.45)
KERNELS = len(FRACTIONS)
FLOOR = 0.5
EVERY = ("band", "patch")
GROUP = 8
PART_ROWS = TILES + TILES_X // 2
LANES = 128
VMEM_LIMIT = 40 << 20
SMALL_LIMIT = 24 << 20


def split_pair(values):
    high = values.astype(jnp.bfloat16)
    low = (values - high.astype(jnp.float32)).astype(jnp.bfloat16)
    return high, low


def kernel_bands(side, taps):
    offset = np.arange(side + 2 * taps)[None, :] - np.arange(side)[:, None]
    inside = (offset >= 0) & (offset <= 2 * taps)
    reach = np.arange(2 * taps + 1) - taps
    stacked = []
    for fraction in FRACTIONS:
        width = fraction * taps
        total = np.exp(-0.5 * (reach / width) ** 2).sum()
        full = np.where(inside, np.exp(-0.5 * ((offset - taps) / width) ** 2) / total, 0.0)
        full = full.astype(np.float32)
        high = full.astype(ml_dtypes.bfloat16)
        low = (full - high.astype(np.float32)).astype(ml_dtypes.bfloat16)
        stacked.append(np.concatenate([high, low, high], axis=1))
    columns = np.concatenate([matrix.T for matrix in stacked], axis=1)
    rows = np.stack(stacked)
    return columns, rows


def cut_rows(flat, values, start, step):
    side = values.shape[-1]
    half = side // 2
    left = lax.broadcasted_iota(jnp.int32, (8, side), 1) < half
    for row in range(0, half, 8):
        upper = values[row : row + 8]
        lower = values[half + row : half + row + 8]
        first = jnp.where(left, upper, pltpu.roll(lower, half, 1))
        second = jnp.where(left, pltpu.roll(upper, half, 1), lower)
        flat[pl.ds(start + 2 * row * step, 8, stride=2 * step), :] = first
        flat[pl.ds(start + (2 * row + 1) * step, 8, stride=2 * step), :] = second


def weight_of(lines, inverse, piece):
    row_index = lax.broadcasted_iota(jnp.int32, inverse.shape, 0)
    lane_index = lax.broadcasted_iota(jnp.int32, inverse.shape, 1)
    masked = (row_index == lines[0, piece]) | (lane_index == lines[1, piece])
    return jnp.where(masked, 0.0, inverse)


def match_body(
    lines, place, owner_ref, tile_ref, image_ref, coeff_ref, inverse_ref, columns_ref, rows_ref, out_ref, *, depth
):
    side = inverse_ref.shape[-1]
    group = pl.program_id(0)
    pieces = depth // 2

    @pl.when(group == 0)
    def _():
        code = (owner_ref[...] * TILES + tile_ref[...]).astype(jnp.float32)
        code = jnp.concatenate([code] * (LANES // pieces), axis=1)
        part = lax.broadcasted_iota(jnp.int32, code.shape, 1) // pieces
        code = jnp.where(part == lax.rem(place[0], LANES // pieces), code, 0.0)
        code = jnp.broadcast_to(code, (8, LANES))
        for slab in range(0, out_ref.shape[0] // depth, 8):
            out_ref[pl.ds(slab * depth + depth - 1, 8, stride=depth), :] = code

    high, low = split_pair(image_ref[...].reshape(-1, image_ref.shape[-1]))
    stacked = jnp.concatenate([high, high, low], axis=1)
    across_all = jnp.dot(stacked, columns_ref[...], preferred_element_type=jnp.float32)

    def one_pair(pair, carry):
        wide = image_ref.shape[-1]
        across = [across_all[(2 * pair + n) * wide : (2 * pair + n + 1) * wide] for n in range(2)]
        matched = None
        for k in range(KERNELS):
            both = jnp.concatenate([part[:, k * side : (k + 1) * side] for part in across], axis=1)
            high = both.astype(jnp.bfloat16).astype(jnp.float32)
            stacked = jnp.concatenate([high, high, both - high], axis=0).astype(jnp.bfloat16)
            smooth = jnp.dot(rows_ref[k], stacked, preferred_element_type=jnp.float32)
            terms = [
                coeff_ref[2 * pair + n, k].astype(jnp.float32) * smooth[:, n * side : (n + 1) * side]
                for n in range(2)
            ]
            matched = terms if matched is None else [a + b for a, b in zip(matched, terms)]
        for n in range(2):
            p = 2 * pair + n
            piece = group * GROUP + p
            weight = weight_of(lines, inverse_ref[p], piece)
            cut_rows(out_ref, weight * matched[n], piece, depth)
            cut_rows(out_ref, weight, pieces + piece, depth)
        return carry

    for pair in range(GROUP // 2):
        one_pair(pair, 0)


def match_pieces(images, coeffs, inverse_var, lines, place, owners, tiles, slabs):
    pieces, wide = images.shape[0], images.shape[-1]
    side = inverse_var.shape[-1]
    depth = 2 * pieces + 1
    columns, rows = kernel_bands(side, (wide - side) // 2)
    kept = (lines, place, owners, tiles, images, coeffs, inverse_var, jnp.asarray(columns), jnp.asarray(rows))
    kept = [pltpu.with_memory_space_constraint(array, pltpu.HBM) for array in kept]
    return pl.pallas_call(
        functools.partial(match_body, depth=depth),
        grid_spec=pltpu.PrefetchScalarGridSpec(
            num_scalar_prefetch=2,
            grid=(pieces // GROUP,),
            in_specs=[
                pl.BlockSpec((1, pieces), lambda g, *_: (0, 0)),
                pl.BlockSpec((1, pieces), lambda g, *_: (0, 0)),
                pl.BlockSpec((GROUP, wide, wide), lambda g, *_: (g, 0, 0)),
                pl.BlockSpec((GROUP, KERNELS, side, side), lambda g, *_: (g, 0, 0, 0)),
                pl.BlockSpec((GROUP, side, side), lambda g, *_: (g, 0, 0)),
                pl.BlockSpec(columns.shape, lambda g, *_: (0, 0)),
                pl.BlockSpec(rows.shape, lambda g, *_: (0, 0, 0)),
            ],
            out_specs=pl.BlockSpec((slabs * depth, LANES), lambda g, *_: (0, 0)),
        ),
        out_shape=jax.ShapeDtypeStruct((slabs * depth, LANES), jnp.float32),
        compiler_params=pltpu.CompilerParams(vmem_limit_bytes=VMEM_LIMIT),
        name="match_pieces",
    )(*kept)


def binned_sum(chosen, values):
    lanes = values.shape[-1]
    pair = jnp.concatenate(split_pair(values), axis=1)
    sums = jnp.dot(chosen, pair, preferred_element_type=jnp.float32)
    return sums[:, :lanes] + sums[:, lanes:]


def sum_body(slab_ref, out_ref, *, depth, bands):
    lanes = slab_ref.shape[-1]
    half = lanes // 2
    pieces = depth // 2
    holders = slab_ref.shape[0] // (depth * bands)
    joined = lanes // pieces
    patches = out_ref.shape[0] // (PART_ROWS * bands)
    bins = lax.broadcasted_iota(jnp.int32, (patches * TILES, lanes), 0)
    total = None
    for band in range(bands):
        starts = [(band * holders + s) * depth for s in range(holders)]

        def plane(first):
            return jnp.concatenate(
                [slab_ref[start + first + m : start + first + m + 8, :] for start in starts for m in range(0, pieces, 8)]
            )

        chosen = []
        for first in range(0, holders, joined):
            code = sum(slab_ref[start + depth - 1 : start + depth, :] for start in starts[first : first + joined])
            chosen.append(jnp.where(bins == code.astype(jnp.int32), 1.0, 0.0).astype(jnp.bfloat16))
        chosen = jnp.concatenate(chosen, axis=1)
        numerator = binned_sum(chosen, plane(0))
        denominator = binned_sum(chosen, plane(pieces))
        coadd = numerator / jnp.maximum(denominator, FLOOR)
        for patch in range(patches):
            start = (band * patches + patch) * PART_ROWS
            out_ref[start : start + TILES, :] = coadd[patch * TILES : (patch + 1) * TILES]
        term = numerator * coadd
        total = term if total is None else total + term
    left = lax.broadcasted_iota(jnp.int32, (TILES_X, lanes), 1) < half
    for patch in range(patches):
        for top in range(TILES_Y):
            first = (patch * TILES_Y + top) * TILES_X
            tiles = total[first : first + TILES_X]
            later = pltpu.roll(tiles, TILES_X // 2, 0)
            upper = jnp.where(left, tiles, pltpu.roll(later, half, 1))
            lower = jnp.where(left, pltpu.roll(tiles, half, 1), later)
            for low, packed in enumerate((upper, lower)):
                start = ((2 * top + low) * patches + patch) * PART_ROWS + TILES
                out_ref[start : start + TILES_X // 2, :] = packed[: TILES_X // 2]


def sum_slabs(slabs, bands, patches, depth):
    rows, lanes = bands * patches * PART_ROWS, slabs.shape[-1]
    return pl.pallas_call(
        functools.partial(sum_body, depth=depth, bands=bands),
        in_specs=[pl.BlockSpec(memory_space=pltpu.VMEM)],
        out_specs=pl.BlockSpec(memory_space=pltpu.VMEM),
        out_shape=jax.ShapeDtypeStruct((rows, lanes), jnp.float32),
        compiler_params=pltpu.CompilerParams(vmem_limit_bytes=SMALL_LIMIT),
        name="sum_slabs",
    )(slabs)


def place_body(part_ref, coadd_ref, detection_ref):
    lanes = part_ref.shape[-1]
    half = lanes // 2
    left = lax.broadcasted_iota(jnp.int32, (8, lanes), 1) < half

    def column(tile):
        return pl.ds(tile % TILES_X * lanes, lanes)

    base = pl.program_id(0) * 2 * coadd_ref.shape[1] * PART_ROWS
    for row in range(0, coadd_ref.shape[1], 8):
        for part in range(PART_ROWS):
            start = base + 2 * row * PART_ROWS + part
            even = part_ref[pl.ds(start, 8, stride=2 * PART_ROWS), :]
            odd = part_ref[pl.ds(start + PART_ROWS, 8, stride=2 * PART_ROWS), :]
            first = jnp.where(left, even, pltpu.roll(odd, half, 1))
            second = jnp.where(left, pltpu.roll(even, half, 1), odd)
            if part < TILES:
                top = 2 * (part // TILES_X)
                coadd_ref[top, row : row + 8, column(part)] = first
                coadd_ref[top + 1, row : row + 8, column(part)] = second
            else:
                detection_ref[row : row + 8, column(part - TILES)] = first
                detection_ref[row : row + 8, column(part - TILES + TILES_X // 2)] = second


def place_parts(parts, side):
    lanes = parts.shape[-1]
    steps = 2
    half = side // 2
    return pl.pallas_call(
        place_body,
        grid=(steps,),
        in_specs=[pl.BlockSpec(memory_space=pltpu.VMEM)],
        out_specs=[
            pl.BlockSpec((2 * TILES_Y, half // steps, TILES_X * lanes), lambda g: (0, g, 0)),
            pl.BlockSpec((half // steps, TILES_X * lanes), lambda g: (g, 0)),
        ],
        out_shape=[
            jax.ShapeDtypeStruct((2 * TILES_Y, half, TILES_X * lanes), jnp.float32),
            jax.ShapeDtypeStruct((half, TILES_X * lanes), jnp.float32),
        ],
        compiler_params=pltpu.CompilerParams(vmem_limit_bytes=SMALL_LIMIT),
        name="place_parts",
    )(parts)


def exchange(rows, devices):
    lanes = rows.shape[-1]
    chunks = rows.reshape(devices, -1, 1, lanes)
    return lax.all_to_all(chunks, EVERY, split_axis=0, concat_axis=0, tiled=True).reshape(-1, lanes)


def per_device(images, coeffs, inverse_var, bad_lines, destinations, tile_slots):
    bands, patches = lax.axis_size("band"), lax.axis_size("patch")
    devices = bands * patches
    pieces, side = inverse_var.shape[1:3]
    lines = bad_lines[0].T
    place = jnp.full((1,), lax.axis_index("patch"), jnp.int32)
    owners = destinations[:, :, 0]
    slabs = match_pieces(images[0], coeffs[0], inverse_var[0], lines, place, owners, tile_slots, devices)
    slabs = exchange(slabs, devices)
    parts = sum_slabs(slabs, bands, patches, 2 * pieces + 1)
    coadd, detection = place_parts(exchange(parts, devices), side)
    return (coadd.reshape(1, 1, TILES_Y * side, TILES_X * side), detection[None])


def solution(mesh):
    in_specs = (
        P("band", "patch", None, None),
        P("band", "patch", None, None, None),
        P("band", "patch", None, None),
        P("band", "patch", None),
        P("band", "patch", None),
        P("band", "patch"),
    )
    out_specs = (P("band", "patch", None, None), P("patch", "band", None))
    return jax.shard_map(
        per_device, mesh=mesh, in_specs=in_specs, out_specs=out_specs, check_vma=False
    )
```

```python
import functools

import jax
import jax.numpy as jnp
import ml_dtypes
import numpy as np
from jax import lax
from jax.experimental import pallas as pl
from jax.experimental.pallas import tpu as pltpu
from jax.sharding import PartitionSpec as P

TILES_X = 8
TILES_Y = 2
TILES = TILES_X * TILES_Y
FRACTIONS = (0.12, 0.25, 0.45)
KERNELS = len(FRACTIONS)
FLOOR = 0.5
EVERY = ("band", "patch")
GROUP = 8
PART_ROWS = TILES + TILES_X // 2
LANES = 128
VMEM_LIMIT = 40 << 20
SMALL_LIMIT = 24 << 20


def split_pair(values):
    high = values.astype(jnp.bfloat16)
    low = (values - high.astype(jnp.float32)).astype(jnp.bfloat16)
    return high, low


def kernel_bands(side, taps):
    offset = np.arange(side + 2 * taps)[None, :] - np.arange(side)[:, None]
    inside = (offset >= 0) & (offset <= 2 * taps)
    reach = np.arange(2 * taps + 1) - taps
    stacked = []
    for fraction in FRACTIONS:
        width = fraction * taps
        total = np.exp(-0.5 * (reach / width) ** 2).sum()
        full = np.where(inside, np.exp(-0.5 * ((offset - taps) / width) ** 2) / total, 0.0)
        full = full.astype(np.float32)
        high = full.astype(ml_dtypes.bfloat16)
        low = (full - high.astype(np.float32)).astype(ml_dtypes.bfloat16)
        stacked.append(np.concatenate([high, low, high], axis=1))
    columns = np.concatenate([matrix.T for matrix in stacked], axis=1)
    rows = np.stack(stacked)
    return columns, rows


def cut_rows(flat, values, start, step):
    side = values.shape[-1]
    half = side // 2
    left = lax.broadcasted_iota(jnp.int32, (8, side), 1) < half
    for row in range(0, half, 8):
        upper = values[row : row + 8]
        lower = values[half + row : half + row + 8]
        first = jnp.where(left, upper, pltpu.roll(lower, half, 1))
        second = jnp.where(left, pltpu.roll(upper, half, 1), lower)
        flat[pl.ds(start + 2 * row * step, 8, stride=2 * step), :] = first
        flat[pl.ds(start + (2 * row + 1) * step, 8, stride=2 * step), :] = second


def weight_of(lines, inverse, piece):
    row_index = lax.broadcasted_iota(jnp.int32, inverse.shape, 0)
    lane_index = lax.broadcasted_iota(jnp.int32, inverse.shape, 1)
    masked = (row_index == lines[0, piece]) | (lane_index == lines[1, piece])
    return jnp.where(masked, 0.0, inverse)


def match_body(
    lines, place, owner_ref, tile_ref, image_ref, coeff_ref, inverse_ref, columns_ref, rows_ref, out_ref, *, depth
):
    side = inverse_ref.shape[-1]
    group = pl.program_id(0)
    pieces = depth // 2

    @pl.when(group == 0)
    def _():
        code = (owner_ref[...] * TILES + tile_ref[...]).astype(jnp.float32)
        code = jnp.concatenate([code] * (LANES // pieces), axis=1)
        part = lax.broadcasted_iota(jnp.int32, code.shape, 1) // pieces
        code = jnp.where(part == lax.rem(place[0], LANES // pieces), code, 0.0)
        code = jnp.broadcast_to(code, (8, LANES))
        for slab in range(0, out_ref.shape[0] // depth, 8):
            out_ref[pl.ds(slab * depth + depth - 1, 8, stride=depth), :] = code

    high, low = split_pair(image_ref[...].reshape(-1, image_ref.shape[-1]))
    stacked = jnp.concatenate([high, high, low], axis=1)
    across_all = jnp.dot(stacked, columns_ref[...], preferred_element_type=jnp.float32)

    def one_pair(pair, carry):
        wide = image_ref.shape[-1]
        across = [across_all[(2 * pair + n) * wide : (2 * pair + n + 1) * wide] for n in range(2)]
        matched = None
        for k in range(KERNELS):
            both = jnp.concatenate([part[:, k * side : (k + 1) * side] for part in across], axis=1)
            high = both.astype(jnp.bfloat16).astype(jnp.float32)
            stacked = jnp.concatenate([high, high, both - high], axis=0).astype(jnp.bfloat16)
            smooth = jnp.dot(rows_ref[k], stacked, preferred_element_type=jnp.float32)
            terms = [
                coeff_ref[2 * pair + n, k].astype(jnp.float32) * smooth[:, n * side : (n + 1) * side]
                for n in range(2)
            ]
            matched = terms if matched is None else [a + b for a, b in zip(matched, terms)]
        for n in range(2):
            p = 2 * pair + n
            piece = group * GROUP + p
            weight = weight_of(lines, inverse_ref[p], piece)
            cut_rows(out_ref, weight * matched[n], piece, depth)
            cut_rows(out_ref, weight, pieces + piece, depth)
        return carry

    for pair in range(GROUP // 2):
        one_pair(pair, 0)


def match_pieces(images, coeffs, inverse_var, lines, place, owners, tiles, slabs):
    pieces, wide = images.shape[0], images.shape[-1]
    side = inverse_var.shape[-1]
    depth = 2 * pieces + 1
    columns, rows = kernel_bands(side, (wide - side) // 2)
    kept = (lines, place, owners, tiles, images, coeffs, inverse_var, jnp.asarray(columns), jnp.asarray(rows))
    kept = [pltpu.with_memory_space_constraint(array, pltpu.HBM) for array in kept]
    return pl.pallas_call(
        functools.partial(match_body, depth=depth),
        grid_spec=pltpu.PrefetchScalarGridSpec(
            num_scalar_prefetch=2,
            grid=(pieces // GROUP,),
            in_specs=[
                pl.BlockSpec((1, pieces), lambda g, *_: (0, 0)),
                pl.BlockSpec((1, pieces), lambda g, *_: (0, 0)),
                pl.BlockSpec((GROUP, wide, wide), lambda g, *_: (g, 0, 0)),
                pl.BlockSpec((GROUP, KERNELS, side, side), lambda g, *_: (g, 0, 0, 0)),
                pl.BlockSpec((GROUP, side, side), lambda g, *_: (g, 0, 0)),
                pl.BlockSpec(columns.shape, lambda g, *_: (0, 0)),
                pl.BlockSpec(rows.shape, lambda g, *_: (0, 0, 0)),
            ],
            out_specs=pl.BlockSpec((slabs * depth, LANES), lambda g, *_: (0, 0)),
        ),
        out_shape=jax.ShapeDtypeStruct((slabs * depth, LANES), jnp.float32),
        compiler_params=pltpu.CompilerParams(vmem_limit_bytes=VMEM_LIMIT),
        name="match_pieces",
    )(*kept)


def binned_sum(chosen, values):
    lanes = values.shape[-1]
    pair = jnp.concatenate(split_pair(values), axis=1)
    sums = jnp.dot(chosen, pair, preferred_element_type=jnp.float32)
    return sums[:, :lanes] + sums[:, lanes:]


def sum_body(slab_ref, out_ref, *, depth, bands):
    lanes = slab_ref.shape[-1]
    half = lanes // 2
    pieces = depth // 2
    holders = slab_ref.shape[0] // (depth * bands)
    joined = lanes // pieces
    patches = out_ref.shape[0] // (PART_ROWS * bands)
    bins = lax.broadcasted_iota(jnp.int32, (patches * TILES, lanes), 0)
    total = None
    for band in range(bands):
        starts = [(band * holders + s) * depth for s in range(holders)]

        def plane(first):
            return jnp.concatenate(
                [slab_ref[start + first + m : start + first + m + 8, :] for start in starts for m in range(0, pieces, 8)]
            )

        chosen = []
        for first in range(0, holders, joined):
            code = sum(slab_ref[start + depth - 1 : start + depth, :] for start in starts[first : first + joined])
            chosen.append(jnp.where(bins == code.astype(jnp.int32), 1.0, 0.0).astype(jnp.bfloat16))
        chosen = jnp.concatenate(chosen, axis=1)
        numerator = binned_sum(chosen, plane(0))
        denominator = binned_sum(chosen, plane(pieces))
        coadd = numerator / jnp.maximum(denominator, FLOOR)
        for patch in range(patches):
            start = (band * patches + patch) * PART_ROWS
            out_ref[start : start + TILES, :] = coadd[patch * TILES : (patch + 1) * TILES]
        term = numerator * coadd
        total = term if total is None else total + term
    left = lax.broadcasted_iota(jnp.int32, (TILES_X, lanes), 1) < half
    for patch in range(patches):
        for top in range(TILES_Y):
            first = (patch * TILES_Y + top) * TILES_X
            tiles = total[first : first + TILES_X]
            later = pltpu.roll(tiles, TILES_X // 2, 0)
            upper = jnp.where(left, tiles, pltpu.roll(later, half, 1))
            lower = jnp.where(left, pltpu.roll(tiles, half, 1), later)
            for low, packed in enumerate((upper, lower)):
                start = ((2 * top + low) * patches + patch) * PART_ROWS + TILES
                out_ref[start : start + TILES_X // 2, :] = packed[: TILES_X // 2]


def sum_slabs(slabs, bands, patches, depth):
    rows, lanes = bands * patches * PART_ROWS, slabs.shape[-1]
    return pl.pallas_call(
        functools.partial(sum_body, depth=depth, bands=bands),
        in_specs=[pl.BlockSpec(memory_space=pltpu.VMEM)],
        out_specs=pl.BlockSpec(memory_space=pltpu.VMEM),
        out_shape=jax.ShapeDtypeStruct((rows, lanes), jnp.float32),
        compiler_params=pltpu.CompilerParams(vmem_limit_bytes=SMALL_LIMIT),
        name="sum_slabs",
    )(slabs)


def place_body(part_ref, coadd_ref, detection_ref):
    lanes = part_ref.shape[-1]
    half = lanes // 2
    left = lax.broadcasted_iota(jnp.int32, (8, lanes), 1) < half

    def column(tile):
        return pl.ds(tile % TILES_X * lanes, lanes)

    base = pl.program_id(0) * 2 * coadd_ref.shape[1] * PART_ROWS
    for row in range(0, coadd_ref.shape[1], 8):
        for part in range(PART_ROWS):
            start = base + 2 * row * PART_ROWS + part
            even = part_ref[pl.ds(start, 8, stride=2 * PART_ROWS), :]
            odd = part_ref[pl.ds(start + PART_ROWS, 8, stride=2 * PART_ROWS), :]
            first = jnp.where(left, even, pltpu.roll(odd, half, 1))
            second = jnp.where(left, pltpu.roll(even, half, 1), odd)
            if part < TILES:
                top = 2 * (part // TILES_X)
                coadd_ref[top, row : row + 8, column(part)] = first
                coadd_ref[top + 1, row : row + 8, column(part)] = second
            else:
                detection_ref[row : row + 8, column(part - TILES)] = first
                detection_ref[row : row + 8, column(part - TILES + TILES_X // 2)] = second


def place_parts(parts, side):
    lanes = parts.shape[-1]
    steps = 1
    half = side // 2
    return pl.pallas_call(
        place_body,
        grid=(steps,),
        in_specs=[pl.BlockSpec(memory_space=pltpu.VMEM)],
        out_specs=[
            pl.BlockSpec((2 * TILES_Y, half // steps, TILES_X * lanes), lambda g: (0, g, 0)),
            pl.BlockSpec((half // steps, TILES_X * lanes), lambda g: (g, 0)),
        ],
        out_shape=[
            jax.ShapeDtypeStruct((2 * TILES_Y, half, TILES_X * lanes), jnp.float32),
            jax.ShapeDtypeStruct((half, TILES_X * lanes), jnp.float32),
        ],
        compiler_params=pltpu.CompilerParams(vmem_limit_bytes=SMALL_LIMIT),
        name="place_parts",
    )(parts)


def exchange(rows, devices):
    lanes = rows.shape[-1]
    chunks = rows.reshape(devices, -1, 1, lanes)
    return lax.all_to_all(chunks, EVERY, split_axis=0, concat_axis=0, tiled=True).reshape(-1, lanes)


def per_device(images, coeffs, inverse_var, bad_lines, destinations, tile_slots):
    bands, patches = lax.axis_size("band"), lax.axis_size("patch")
    devices = bands * patches
    pieces, side = inverse_var.shape[1:3]
    lines = bad_lines[0].T
    place = jnp.full((1,), lax.axis_index("patch"), jnp.int32)
    owners = destinations[:, :, 0]
    slabs = match_pieces(images[0], coeffs[0], inverse_var[0], lines, place, owners, tile_slots, devices)
    slabs = exchange(slabs, devices)
    parts = sum_slabs(slabs, bands, patches, 2 * pieces + 1)
    coadd, detection = place_parts(exchange(parts, devices), side)
    return (coadd.reshape(1, 1, TILES_Y * side, TILES_X * side), detection[None])


def solution(mesh):
    in_specs = (
        P("band", "patch", None, None),
        P("band", "patch", None, None, None),
        P("band", "patch", None, None),
        P("band", "patch", None),
        P("band", "patch", None),
        P("band", "patch"),
    )
    out_specs = (P("band", "patch", None, None), P("patch", "band", None))
    return jax.shard_map(
        per_device, mesh=mesh, in_specs=in_specs, out_specs=out_specs, check_vma=False
    )
```
